32 devices in a mesh: seq: 8 (over y, x, core), vid: 4 (over z).
Axes of the slice: x: 2, y: 2, z: 4, core: 2. Of those that a mesh axis runs over, the one named last changes fastest.
Arguments:
- tokens: bfloat16 [32768, 768], P(('vid', 'seq')), parts along dimension 0, may hold values from -100 to 100
- latents: bfloat16 [2048, 768], P(('vid', 'seq')), parts along dimension 0, may hold values from -6 to 6
- read_weights: bfloat16 [4, 768, 768], P(None, 'seq'), may hold values from -1 to 1
- later_weights: bfloat16 [8, 768, 768], P(None, 'seq'), may hold values from -1 to 1
- head_scale: float32 [3, 12], replicated, may hold values from 1 to 40
Outputs:
- tokens_out: bfloat16 [32768, 768], P(('vid', 'seq')), parts along dimension 0
- latents_out: float32 [2048, 768], P(('vid', 'seq')), parts along dimension 0
The draws below stay inside these ranges and needn't reach their ends.
There are 4 independent parts, one for each index of `vid`. The reference program is written for one: setup_inputs(seed, part) draws one part's arguments, and reference() takes and returns one part's arrays. A program takes and returns all parts, laid end to end along the dimension named above; an argument that names none is the same for every part. Nothing has to cross between parts.
All inputs are finite; a program needn't handle non-finite values.
Results may differ from the reference program's by a relative error of at most 0.01.
The reference program's roundings to bfloat16 on the way count: a program that leaves them out, or rounds other values in their place, can miss the bound.
Values may be sent and summed in bfloat16 or wider, within the bound.
A program may use at most 64 MiB of HBM per device.

```python
import math
import jax
import jax.numpy as jnp
from jax import lax

D = 768
HEADS = 12
LATENTS = 512
TOK_DEV = 1024
TOKENS = 8192


def latent_base(key):
    return jnp.clip(jax.random.normal(jax.random.fold_in(key, 11), (LATENTS, D), jnp.float32), -6.0, 6.0)


def draw_latents(key, part):
    return latent_base(key).astype(jnp.bfloat16)


def draw_tokens(key, part):
    slab_count = TOKENS // TOK_DEV
    slab_amp = jnp.exp(jax.random.uniform(jax.random.fold_in(key, 3), (slab_count, 1), jnp.float32, math.log(0.3), math.log(3.0)))
    centre = jax.random.normal(jax.random.fold_in(key, 4), (slab_count, D), jnp.float32) * slab_amp
    noise_rows = jax.random.normal(jax.random.fold_in(key, 5), (slab_count, TOK_DEV, D), jnp.float32)
    values = noise_rows + centre[:, None, :]
    return jnp.clip(values.reshape(TOKENS, D), -100.0, 100.0).astype(jnp.bfloat16)


def weight_stack(key, count):
    matrices = jax.random.normal(key, (count, D, D), jnp.float32) / math.sqrt(D)
    return jnp.clip(matrices, -6.0 / math.sqrt(D), 6.0 / math.sqrt(D))


def draw_read_weights(key, part):
    matrices = weight_stack(jax.random.fold_in(key, 21), 4)
    return matrices.astype(jnp.bfloat16)


def draw_later_weights(key, part):
    matrices = weight_stack(jax.random.fold_in(key, 22), 8)
    return matrices.astype(jnp.bfloat16)


def draw_head_scale(key, part):
    values = jnp.exp(jax.random.uniform(jax.random.fold_in(key, 31), (3, HEADS), jnp.float32, 0.0, math.log(4.0)))
    return values


def setup_inputs(seed: int = 0, part: int = 0) -> dict:
    seeds = jax.random.split(jax.random.key(seed), 6)
    own_keys = jax.random.split(jax.random.fold_in(seeds[5], part), 6)
    tokens = draw_tokens(jax.random.fold_in(jax.random.fold_in(seeds[5], part), 71), part)
    latents = draw_latents(jax.random.fold_in(jax.random.fold_in(seeds[5], part), 71), part)
    read_weights = draw_read_weights(jax.random.fold_in(seeds[5], 71), part)
    later_weights = draw_later_weights(jax.random.fold_in(seeds[5], 71), part)
    head_scale = draw_head_scale(jax.random.fold_in(seeds[5], 71), part)
    return {"tokens": tokens, "latents": latents, "read_weights": read_weights, "later_weights": later_weights, "head_scale": head_scale}


epsilon = 1e-06

def norm_rows(values):
    values = values.astype(jnp.float32)
    return values * lax.rsqrt(lax.optimization_barrier(jnp.mean(values * values, axis=-1, keepdims=True)) + epsilon)

def head_norm(values, n_heads):
    by_head = values.reshape(values.shape[0], n_heads, values.shape[1] // n_heads)
    by_head = by_head * lax.rsqrt(lax.optimization_barrier(jnp.mean(by_head * by_head, axis=-1, keepdims=True)) + epsilon)
    return by_head.reshape(values.shape).astype(jnp.bfloat16)

def project(inputs, weight):
    return jnp.dot(inputs, weight, preferred_element_type=jnp.float32)

def head_cols(values, head_index, head_dim):
    return lax.dynamic_slice_in_dim(values, head_index * head_dim, head_dim, 1)

def inner(left, right):
    return lax.dot_general(left, right, (((1,), (1,)), ((), ())), preferred_element_type=jnp.float32)

def attend(queries, key_rows, val_rows, factors, n_heads):
    head_dim = queries.shape[1] // n_heads

    def one_head(packed):
        head_index, factor = packed
        scores = inner(head_cols(queries, head_index, head_dim), head_cols(key_rows, head_index, head_dim)) * (factor / math.sqrt(head_dim))
        row_top = lax.optimization_barrier(jnp.max(scores, axis=1, keepdims=True))
        exp_scores = jnp.exp(scores - row_top)
        weights = (exp_scores / lax.optimization_barrier(jnp.sum(exp_scores, axis=1, keepdims=True))).astype(jnp.bfloat16)
        return jnp.dot(weights, head_cols(val_rows, head_index, head_dim), preferred_element_type=jnp.float32)
    results = lax.map(one_head, (jnp.arange(n_heads, dtype=jnp.int32), factors))
    return results.transpose(1, 0, 2).reshape(queries.shape).astype(jnp.bfloat16)

def read_parts(queries, key_rows, val_rows, factors, n_heads):
    head_dim = queries.shape[1] // n_heads

    def one_head(packed):
        head_index, factor = packed
        scores = inner(head_cols(queries, head_index, head_dim), head_cols(key_rows, head_index, head_dim)) * (factor / math.sqrt(head_dim))
        row_top = lax.optimization_barrier(jnp.max(scores, axis=1))
        exp_scores = jnp.exp(scores - row_top[:, None])
        totals = lax.optimization_barrier(jnp.sum(exp_scores, axis=1))
        summed = jnp.dot(exp_scores.astype(jnp.bfloat16), head_cols(val_rows, head_index, head_dim), preferred_element_type=jnp.float32)
        return (summed.astype(jnp.bfloat16), row_top, totals)
    return lax.map(one_head, (jnp.arange(n_heads, dtype=jnp.int32), factors))

def reference(tokens, latents, read_weights, later_weights, head_scale):
    tok_normed = norm_rows(tokens).astype(jnp.bfloat16)
    read_q = head_norm(project(norm_rows(latents).astype(jnp.bfloat16), read_weights[0]), HEADS)
    read_k = head_norm(project(tok_normed, read_weights[1]), HEADS)
    read_v = project(tok_normed, read_weights[2]).astype(jnp.bfloat16)
    slab_count = TOKENS // TOK_DEV
    key_slabs = read_k.reshape(slab_count, TOK_DEV, D)
    val_slabs = read_v.reshape(slab_count, TOK_DEV, D)

    def one_slab(slab_pair):
        return read_parts(read_q, slab_pair[0], slab_pair[1], head_scale[0], HEADS)
    partials, row_tops, totals = lax.map(one_slab, (key_slabs, val_slabs))
    row_best = lax.optimization_barrier(jnp.max(row_tops, axis=0))
    rescale = jnp.exp(row_tops - row_best[None])
    summed = lax.optimization_barrier(jnp.sum(partials.astype(jnp.float32) * rescale[..., None], axis=0))
    weight_sum = lax.optimization_barrier(jnp.sum(totals * rescale, axis=0))
    read_mixed = summed / weight_sum[..., None]
    read_mix = read_mixed.transpose(1, 0, 2).reshape(LATENTS, D).astype(jnp.bfloat16)
    lat_one = latents.astype(jnp.float32) + project(read_mix, read_weights[3])
    self_normed = norm_rows(lat_one).astype(jnp.bfloat16)
    self_q = head_norm(project(self_normed, later_weights[0]), HEADS)
    self_k = head_norm(project(self_normed, later_weights[1]), HEADS)
    self_v = project(self_normed, later_weights[2]).astype(jnp.bfloat16)
    latents_out = lat_one + project(attend(self_q, self_k, self_v, head_scale[1], HEADS), later_weights[3])
    write_in = norm_rows(latents_out).astype(jnp.bfloat16)
    write_q = head_norm(project(tok_normed, later_weights[4]), HEADS)
    write_k = head_norm(project(write_in, later_weights[5]), HEADS)
    write_v = project(write_in, later_weights[6]).astype(jnp.bfloat16)
    tokens_out = (tokens.astype(jnp.float32) + project(attend(write_q, write_k, write_v, head_scale[2], HEADS), later_weights[7])).astype(jnp.bfloat16)
    return (tokens_out, latents_out)
```

```python
import functools
import math

import jax
import jax.numpy as jnp
from jax import lax
from jax.experimental import pallas as pl
from jax.experimental.pallas import tpu as pltpu
from jax.sharding import PartitionSpec as P

HEADS = 12
LANES = 128
epsilon = 1e-06
LOG2E = math.log2(math.e)
BF16 = jnp.bfloat16
F32 = jnp.float32


def rms(values):
    return values * lax.rsqrt(jnp.mean(values * values, axis=-1, keepdims=True) + epsilon)


def dot(left, right):
    return jnp.dot(left, right, preferred_element_type=F32)


def inner(left, right):
    return lax.dot_general(left, right, (((1,), (1,)), ((), ())), preferred_element_type=F32)


def group_matrix(head_dim):
    size = 2 * LANES
    row = lax.broadcasted_iota(jnp.int32, (size, size), 0) // head_dim
    col = lax.broadcasted_iota(jnp.int32, (size, size), 1) // head_dim
    return jnp.where(row == col, 1.0 / head_dim, 0.0).astype(BF16)


def head_norm(values, group):
    size = group.shape[0]
    parts = []
    for start in range(0, values.shape[1], size):
        block = values[:, start : start + size]
        square = block * block
        high = square.astype(BF16)
        low = (square - high.astype(F32)).astype(BF16)
        mean = dot(high, group) + dot(low, group)
        parts.append((block * lax.rsqrt(mean + epsilon)).astype(BF16))
    return jnp.concatenate(parts, axis=1)


def by_rows(rows, chunk, body):
    chunk = min(chunk, rows)

    def step(index, carry):
        body(pl.ds(pl.multiple_of(index * chunk, chunk), chunk))
        return carry

    lax.fori_loop(0, rows // chunk, step, 0)


def half_masks(head_dim):
    lane = lax.broadcasted_iota(jnp.int32, (1, LANES), 1) // head_dim
    return [(lane == part).astype(F32).astype(BF16) for part in range(LANES // head_dim)]


def merge_halves(parts, head_dim):
    lane = lax.broadcasted_iota(jnp.int32, parts[0].shape, 1) // head_dim
    result = parts[0]
    for part in range(1, len(parts)):
        result = jnp.where(lane == part, parts[part], result)
    return result


def attention(q_ref, k_ref, v_ref, scale_ref, which, out_ref, stats_ref, chunk):
    rows, width = q_ref.shape
    head_dim = width // HEADS
    per_block = LANES // head_dim
    chunk = min(chunk, rows)
    n_chunks = rows // chunk
    masks = half_masks(head_dim)
    root = 1.0 / math.sqrt(head_dim)

    def step(index, carry):
        block = index // n_chunks
        part = index % n_chunks
        cols = pl.ds(pl.multiple_of(block * LANES, LANES), LANES)
        here = pl.ds(pl.multiple_of(part * chunk, chunk), chunk)
        q = q_ref[here, cols]
        k = k_ref[:, cols]
        v = v_ref[:, cols]
        results = []
        for half in range(per_block):
            head = block * per_block + half
            factor = scale_ref[which, head] * root
            scores = inner(q * masks[half], k)
            top = jnp.max(scores, axis=1, keepdims=True)
            exp_scores = jnp.exp2((scores - top) * (factor * LOG2E))
            total = jnp.sum(exp_scores, axis=1, keepdims=True)
            if stats_ref is None:
                weights = (exp_scores * (1.0 / total)).astype(BF16)
            else:
                weights = exp_scores.astype(BF16)
                lane = lax.broadcasted_iota(jnp.int32, (chunk, LANES), 1)
                old = stats_ref[here, :]
                old = jnp.where(lane == head, top * factor, old)
                stats_ref[here, :] = jnp.where(lane == head + LANES // 2, total, old)
            results.append(dot(weights, v))
        out_ref[here, cols] = merge_halves(results, head_dim).astype(BF16)
        return carry

    lax.fori_loop(0, (width // LANES) * n_chunks, step, 0)


def read_body(tok_ref, lat_ref, w_ref, scale_ref, parts_ref, stats_ref, q_ref, k_ref, v_ref):
    group = group_matrix(tok_ref.shape[1] // HEADS)

    def latent_rows(here):
        normed = rms(lat_ref[here, :].astype(F32)).astype(BF16)
        q_ref[here, :] = head_norm(dot(normed, w_ref[0]), group)

    def token_rows(here):
        normed = rms(tok_ref[here, :].astype(F32)).astype(BF16)
        k_ref[here, :] = head_norm(dot(normed, w_ref[1]), group)
        v_ref[here, :] = dot(normed, w_ref[2]).astype(BF16)

    by_rows(lat_ref.shape[0], 256, latent_rows)
    by_rows(tok_ref.shape[0], 256, token_rows)
    attention(q_ref, k_ref, v_ref, scale_ref, 0, parts_ref, stats_ref, 256)


def combine_body(got_ref, stats_ref, lat_ref, out_w_ref, w_ref, one_ref, q_ref, kv_ref):
    count, rows, width = got_ref.shape
    head_dim = width // HEADS
    group = group_matrix(head_dim)
    per_block = LANES // head_dim
    stats = [stats_ref[b] for b in range(count)]
    best = functools.reduce(jnp.maximum, stats)
    rescale = [jnp.exp(item - best) for item in stats]
    half = LANES // 2
    bottom = sum(rescale[b][:, :half] * stats[b][:, half:] for b in range(count))
    inverse = 1.0 / bottom
    mixed = []
    for block in range(width // LANES):
        cols = slice(block * LANES, block * LANES + LANES)
        total = jnp.zeros((rows, LANES), F32)
        heads = range(block * per_block, block * per_block + per_block)

        def spread(values):
            return merge_halves(
                [jnp.broadcast_to(values[:, h : h + 1], (rows, LANES)) for h in heads], head_dim
            )

        for b in range(count):
            total += got_ref[b, :, cols].astype(F32) * spread(rescale[b])
        mixed.append((total * spread(inverse)).astype(BF16))
    read_mix = jnp.concatenate(mixed, axis=1)
    lat_one = lat_ref[...].astype(F32) + dot(read_mix, out_w_ref[...])
    one_ref[...] = lat_one
    normed = rms(lat_one).astype(BF16)
    q_ref[...] = head_norm(dot(normed, w_ref[0]), group)
    kv_ref[:, :width] = head_norm(dot(normed, w_ref[1]), group)
    kv_ref[:, width:] = dot(normed, w_ref[2]).astype(BF16)


def self_body(one_ref, q_ref, kv_ref, w_ref, scale_ref, out_ref, in_ref, mix_ref):
    width = one_ref.shape[1]
    attention(
        q_ref, kv_ref.at[:, :width], kv_ref.at[:, width:], scale_ref, 1, mix_ref, None, 64
    )
    latents_out = one_ref[...] + dot(mix_ref[...], w_ref[...])
    out_ref[...] = latents_out
    in_ref[...] = rms(latents_out).astype(BF16)


def write_body(tok_ref, in_ref, w_ref, scale_ref, out_ref, q_ref, k_ref, v_ref, mix_ref):
    group = group_matrix(tok_ref.shape[1] // HEADS)

    def latent_rows(here):
        k_ref[here, :] = head_norm(dot(in_ref[here, :], w_ref[1]), group)
        v_ref[here, :] = dot(in_ref[here, :], w_ref[2]).astype(BF16)

    def token_rows(here):
        normed = rms(tok_ref[here, :].astype(F32)).astype(BF16)
        q_ref[here, :] = head_norm(dot(normed, w_ref[0]), group)

    def out_rows(here):
        out_ref[here, :] = (
            tok_ref[here, :].astype(F32) + dot(mix_ref[here, :], w_ref[3])
        ).astype(out_ref.dtype)

    by_rows(in_ref.shape[0], 256, latent_rows)
    by_rows(tok_ref.shape[0], 256, token_rows)
    attention(q_ref, k_ref, v_ref, scale_ref, 2, mix_ref, None, 256)
    by_rows(tok_ref.shape[0], 256, out_rows)


VM = pl.BlockSpec(memory_space=pltpu.VMEM)
SM = pl.BlockSpec(memory_space=pltpu.SMEM)


def call(body, in_specs, outs, scratch, *args):
    return pl.pallas_call(
        body,
        out_shape=[jax.ShapeDtypeStruct(shape, dtype) for shape, dtype in outs],
        in_specs=in_specs,
        out_specs=[VM] * len(outs),
        scratch_shapes=[pltpu.VMEM(shape, dtype) for shape, dtype in scratch],
        compiler_params=pltpu.CompilerParams(vmem_limit_bytes=56 * 1024 * 1024),
    )(*args)


def gathered(count, tokens, latents, read_weights, later_weights, head_scale):
    own, width = latents.shape
    rows = own * count
    slab = tokens.shape[0]
    read_full = lax.all_gather(read_weights, "seq", axis=1, tiled=True)
    later_full = lax.all_gather(later_weights, "seq", axis=1, tiled=True)
    lat_all = lax.all_gather(latents, "seq", axis=0, tiled=True)
    parts, stats = call(
        read_body,
        [VM, VM, VM, SM],
        [((rows, width), BF16), ((rows, LANES), F32)],
        [((rows, width), BF16), ((slab, width), BF16), ((slab, width), BF16)],
        tokens, lat_all, read_full[:3], head_scale,
    )
    got_parts = lax.all_to_all(
        parts.reshape(count, own, width), "seq", split_axis=0, concat_axis=0, tiled=True
    )
    got_stats = lax.all_to_all(
        stats.reshape(count, own, LANES), "seq", split_axis=0, concat_axis=0, tiled=True
    )
    lat_one, self_q, self_kv = call(
        combine_body,
        [VM] * 5,
        [((own, width), F32), ((own, width), BF16), ((own, 2 * width), BF16)],
        [],
        got_parts, got_stats, latents, read_full[3], later_full[:3],
    )
    all_kv = lax.all_gather(self_kv, "seq", axis=0, tiled=True)
    latents_out, write_in = call(
        self_body,
        [VM, VM, VM, VM, SM],
        [((own, width), F32), ((own, width), BF16)],
        [((own, width), BF16)],
        lat_one, self_q, all_kv, later_full[3], head_scale,
    )
    write_all = lax.all_gather(write_in, "seq", axis=0, tiled=True)
    (tokens_out,) = call(
        write_body,
        [VM, VM, VM, SM],
        [((slab, width), BF16)],
        [((slab, width), BF16), ((rows, width), BF16), ((rows, width), BF16), ((slab, width), BF16)],
        tokens, write_all, later_full[4:], head_scale,
    )
    return tokens_out, latents_out


def solution(mesh):
    placed = (
        P(("vid", "seq"), None),
        P(("vid", "seq"), None),
        P(None, "seq", None),
        P(None, "seq", None),
        P(),
    )
    return jax.shard_map(
        functools.partial(gathered, mesh.shape["seq"]),
        mesh=mesh,
        in_specs=placed,
        out_specs=(P(("vid", "seq"), None), P(("vid", "seq"), None)),
        check_vma=False,
    )
```

```python
import functools
import math

import jax
import jax.numpy as jnp
from jax import lax
from jax.experimental import pallas as pl
from jax.experimental.pallas import tpu as pltpu
from jax.sharding import PartitionSpec as P

HEADS = 12
LANES = 128
epsilon = 1e-06
LOG2E = math.log2(math.e)
BF16 = jnp.bfloat16
F32 = jnp.float32


def rms(values):
    return values * lax.rsqrt(jnp.mean(values * values, axis=-1, keepdims=True) + epsilon)


def dot(left, right):
    return jnp.dot(left, right, preferred_element_type=F32)


def inner(left, right):
    return lax.dot_general(left, right, (((1,), (1,)), ((), ())), preferred_element_type=F32)


def group_matrix(head_dim):
    size = 2 * LANES
    row = lax.broadcasted_iota(jnp.int32, (size, size), 0) // head_dim
    col = lax.broadcasted_iota(jnp.int32, (size, size), 1) // head_dim
    return jnp.where(row == col, 1.0 / head_dim, 0.0).astype(BF16)


def head_norm(values, group):
    size = group.shape[0]
    parts = []
    for start in range(0, values.shape[1], size):
        block = values[:, start : start + size]
        square = block * block
        high = square.astype(BF16)
        low = (square - high.astype(F32)).astype(BF16)
        mean = dot(high, group) + dot(low, group)
        parts.append((block * lax.rsqrt(mean + epsilon)).astype(BF16))
    return jnp.concatenate(parts, axis=1)


def by_rows(rows, chunk, body):
    chunk = min(chunk, rows)

    def step(index, carry):
        body(pl.ds(pl.multiple_of(index * chunk, chunk), chunk))
        return carry

    lax.fori_loop(0, rows // chunk, step, 0)


def half_masks(head_dim):
    lane = lax.broadcasted_iota(jnp.int32, (1, LANES), 1) // head_dim
    return [(lane == part).astype(F32).astype(BF16) for part in range(LANES // head_dim)]


def merge_halves(parts, head_dim):
    lane = lax.broadcasted_iota(jnp.int32, parts[0].shape, 1) // head_dim
    result = parts[0]
    for part in range(1, len(parts)):
        result = jnp.where(lane == part, parts[part], result)
    return result


def attention(q_ref, k_ref, v_ref, scale_ref, which, out_ref, stats_ref, chunk, hooks=None):
    rows, width = q_ref.shape
    head_dim = width // HEADS
    per_block = LANES // head_dim
    chunk = min(chunk, rows)
    n_chunks = rows // chunk
    masks = half_masks(head_dim)
    root = 1.0 / math.sqrt(head_dim)

    def step(index, carry):
        for when, action in (hooks or {}).items():
            pl.when(index == when)(action)
        block = index // n_chunks
        part = index % n_chunks
        cols = pl.ds(pl.multiple_of(block * LANES, LANES), LANES)
        here = pl.ds(pl.multiple_of(part * chunk, chunk), chunk)
        q = q_ref[here, cols]
        k = k_ref[:, cols]
        v = v_ref[:, cols]
        results = []
        for half in range(per_block):
            head = block * per_block + half
            factor = scale_ref[which, head] * root
            scores = inner(q * masks[half], k)
            top = jnp.max(scores, axis=1, keepdims=True)
            exp_scores = jnp.exp2((scores - top) * (factor * LOG2E))
            total = jnp.sum(exp_scores, axis=1, keepdims=True)
            if stats_ref is None:
                weights = (exp_scores * (1.0 / total)).astype(BF16)
            else:
                weights = exp_scores.astype(BF16)
                lane = lax.broadcasted_iota(jnp.int32, (chunk, LANES), 1)
                old = stats_ref[here, :]
                old = jnp.where(lane == head, top * factor, old)
                stats_ref[here, :] = jnp.where(lane == head + LANES // 2, total, old)
            results.append(dot(weights, v))
        out_ref[here, cols] = merge_halves(results, head_dim).astype(BF16)
        return carry

    lax.fori_loop(0, (width // LANES) * n_chunks, step, 0)


def read_body(tok_ref, lat_ref, w_ref, scale_ref, parts_ref, stats_ref, q_ref, k_ref, v_ref):
    group = group_matrix(tok_ref.shape[1] // HEADS)

    stats_ref[...] = jnp.zeros(stats_ref.shape, F32)

    def latent_rows(here):
        normed = rms(lat_ref[here, :].astype(F32)).astype(BF16)
        q_ref[here, :] = head_norm(dot(normed, w_ref[0]), group)

    def token_rows(here):
        normed = rms(tok_ref[here, :].astype(F32)).astype(BF16)
        k_ref[here, :] = head_norm(dot(normed, w_ref[1]), group)
        v_ref[here, :] = dot(normed, w_ref[2]).astype(BF16)

    by_rows(lat_ref.shape[0], 256, latent_rows)
    by_rows(tok_ref.shape[0], 256, token_rows)
    attention(q_ref, k_ref, v_ref, scale_ref, 0, parts_ref, stats_ref, 256)


def combine(got, stats, lat_ref, out_w_ref, w_refs, one_ref, q_ref, kv_ref):
    count = len(got)
    rows, width = got[0].shape
    head_dim = width // HEADS
    group = group_matrix(head_dim)
    per_block = LANES // head_dim
    best = functools.reduce(jnp.maximum, stats)
    rescale = [jnp.exp(item - best) for item in stats]
    half = LANES // 2
    bottom = sum(rescale[b][:, :half] * stats[b][:, half:] for b in range(count))
    inverse = 1.0 / bottom
    mixed = []
    for block in range(width // LANES):
        cols = slice(block * LANES, block * LANES + LANES)
        total = jnp.zeros((rows, LANES), F32)
        heads = range(block * per_block, block * per_block + per_block)

        def spread(values):
            return merge_halves(
                [jnp.broadcast_to(values[:, h : h + 1], (rows, LANES)) for h in heads], head_dim
            )

        for b in range(count):
            total += got[b][:, cols].astype(F32) * spread(rescale[b])
        mixed.append((total * spread(inverse)).astype(BF16))
    read_mix = jnp.concatenate(mixed, axis=1)
    lat_one = lat_ref[...].astype(F32) + dot(read_mix, out_w_ref[...])
    one_ref[...] = lat_one
    normed = rms(lat_one).astype(BF16)
    q_ref[...] = head_norm(dot(normed, w_refs[0][...]), group)
    kv_ref[:, :width] = head_norm(dot(normed, w_refs[1][...]), group)
    kv_ref[:, width:] = dot(normed, w_refs[2][...]).astype(BF16)


def combine_body(got_ref, stats_ref, lat_ref, out_w_ref, w_ref, one_ref, q_ref, kv_ref):
    count = got_ref.shape[0]
    combine(
        [got_ref[b] for b in range(count)],
        [stats_ref[b] for b in range(count)],
        lat_ref, out_w_ref, [w_ref.at[i] for i in range(3)], one_ref, q_ref, kv_ref,
    )


def self_body(one_ref, q_ref, kv_ref, w_ref, scale_ref, out_ref, in_ref, mix_ref):
    width = one_ref.shape[1]
    attention(
        q_ref, kv_ref.at[:, :width], kv_ref.at[:, width:], scale_ref, 1, mix_ref, None, 64
    )
    latents_out = one_ref[...] + dot(mix_ref[...], w_ref[...])
    out_ref[...] = latents_out
    in_ref[...] = rms(latents_out).astype(BF16)


def write_body(tok_ref, in_ref, w_ref, scale_ref, out_ref, q_ref, k_ref, v_ref, mix_ref):
    group = group_matrix(tok_ref.shape[1] // HEADS)

    def latent_rows(here):
        k_ref[here, :] = head_norm(dot(in_ref[here, :], w_ref[1]), group)
        v_ref[here, :] = dot(in_ref[here, :], w_ref[2]).astype(BF16)

    def token_rows(here):
        normed = rms(tok_ref[here, :].astype(F32)).astype(BF16)
        q_ref[here, :] = head_norm(dot(normed, w_ref[0]), group)

    def out_rows(here):
        out_ref[here, :] = (
            tok_ref[here, :].astype(F32) + dot(mix_ref[here, :], w_ref[3])
        ).astype(out_ref.dtype)

    by_rows(in_ref.shape[0], 256, latent_rows)
    by_rows(tok_ref.shape[0], 256, token_rows)
    attention(q_ref, k_ref, v_ref, scale_ref, 2, mix_ref, None, 256)
    by_rows(tok_ref.shape[0], 256, out_rows)


VM = pl.BlockSpec(memory_space=pltpu.VMEM)
SM = pl.BlockSpec(memory_space=pltpu.SMEM)


def call(body, in_specs, outs, scratch, *args):
    return pl.pallas_call(
        body,
        out_shape=[jax.ShapeDtypeStruct(shape, dtype) for shape, dtype in outs],
        in_specs=in_specs,
        out_specs=[VM] * len(outs),
        scratch_shapes=[pltpu.VMEM(shape, dtype) for shape, dtype in scratch],
        compiler_params=pltpu.CompilerParams(vmem_limit_bytes=56 * 1024 * 1024),
    )(*args)


def gathered(count, tokens, latents, read_weights, later_weights, head_scale):
    own, width = latents.shape
    rows = own * count
    slab = tokens.shape[0]
    read_full = lax.all_gather(read_weights, "seq", axis=1, tiled=True)
    later_full = lax.all_gather(later_weights, "seq", axis=1, tiled=True)
    lat_all = lax.all_gather(latents, "seq", axis=0, tiled=True)
    parts, stats = call(
        read_body,
        [VM, VM, VM, SM],
        [((rows, width), BF16), ((rows, LANES), F32)],
        [((rows, width), BF16), ((slab, width), BF16), ((slab, width), BF16)],
        tokens, lat_all, read_full[:3], head_scale,
    )
    got_parts = lax.all_to_all(
        parts.reshape(count, own, width), "seq", split_axis=0, concat_axis=0, tiled=True
    )
    got_stats = lax.all_to_all(
        stats.reshape(count, own, LANES), "seq", split_axis=0, concat_axis=0, tiled=True
    )
    lat_one, self_q, self_kv = call(
        combine_body,
        [VM] * 5,
        [((own, width), F32), ((own, width), BF16), ((own, 2 * width), BF16)],
        [],
        got_parts, got_stats, latents, read_full[3], later_full[:3],
    )
    all_kv = lax.all_gather(self_kv, "seq", axis=0, tiled=True)
    latents_out, write_in = call(
        self_body,
        [VM, VM, VM, VM, SM],
        [((own, width), F32), ((own, width), BF16)],
        [((own, width), BF16)],
        lat_one, self_q, all_kv, later_full[3], head_scale,
    )
    write_all = lax.all_gather(write_in, "seq", axis=0, tiled=True)
    (tokens_out,) = call(
        write_body,
        [VM, VM, VM, SM],
        [((slab, width), BF16)],
        [((slab, width), BF16), ((rows, width), BF16), ((rows, width), BF16), ((slab, width), BF16)],
        tokens, write_all, later_full[4:], head_scale,
    )
    return tokens_out, latents_out


class Gather:
    def __init__(self, source, place, rows, sems, item, spots):
        send, recv = sems
        me, core, along_x, along_y, diagonal = spots
        half = rows // 2
        self.done = set()

        def copy(kind, src, dst, target):
            return pltpu.make_async_remote_copy(
                src_ref=src,
                dst_ref=dst,
                send_sem=send.at[item, kind],
                recv_sem=recv.at[item, kind],
                device_id={"seq": target},
                device_id_type=pl.DeviceIdType.MESH,
            )

        def block(owner, start=0, size=rows):
            return place(pl.ds(pl.multiple_of(owner * rows + start, half), size))

        mine = source if source is not None else block(me)
        self.first = [
            copy(0, mine, block(me), along_x),
            copy(1, mine, block(me), along_y),
            copy(2, mine, block(me), core),
        ]
        self.relay = [
            copy(3, block(along_x, 0, half), block(along_x, 0, half), along_y),
            copy(4, block(along_y, half, half), block(along_y, half, half), along_x),
            copy(5, block(along_x), block(along_x), core),
            copy(6, block(along_y), block(along_y), core),
        ]
        self.last = [copy(7, block(diagonal), block(diagonal), core)]
        self.local = None
        if source is not None:
            self.local = pltpu.make_async_copy(source, block(me), send.at[item, 8])

    def start(self):
        if "start" not in self.done:
            self.done.add("start")
            for copy in self.first:
                copy.start()
            if self.local is not None:
                self.local.start()

    def spread(self):
        if "spread" not in self.done:
            self.done.add("spread")
            self.first[0].wait_recv()
            self.relay[0].start()
            self.relay[2].start()
            self.first[1].wait_recv()
            self.relay[1].start()
            self.relay[3].start()

    def close(self):
        if "close" not in self.done:
            self.done.add("close")
            self.relay[0].wait_recv()
            self.relay[1].wait_recv()
            self.last[0].start()

    def need(self):
        self.spread()
        self.close()
        self.first[2].wait_recv()
        self.relay[2].wait_recv()
        self.relay[3].wait_recv()
        self.last[0].wait_recv()
        if self.local is not None:
            self.local.wait()

    def drain(self):
        for copy in self.first + self.relay + self.last:
            copy.wait_send()


def whole_body(
    count, tok_ref, lat_ref, rw_ref, lw_ref, scale_ref, out_ref, lat_out_ref,
    w_ref, norm_ref, lat_all, q_ref, k_ref, v_ref, parts_ref, stats_ref,
    got_ref, got_stats, one_ref, self_q, kv_ref, mix_small, in_ref,
    wq_ref, wk_ref, wv_ref, mix_ref, send, recv, slab_send, slab_recv,
):
    me = lax.axis_index("seq")
    core = me + 1 - 2 * (me % 2)
    along_x = me + 2 - 4 * ((me // 2) % 2)
    along_y = me + 4 - 8 * (me // 4)
    diagonal = along_x + 4 - 8 * (me // 4)
    spots = (me, core, along_x, along_y, diagonal)
    own, width = lat_ref.shape
    n_read = rw_ref.shape[0]
    shard = rw_ref.shape[1]
    group = group_matrix(width // HEADS)
    sems = (send, recv)

    barrier = pltpu.get_barrier_semaphore()
    for step in range(1, count):
        pl.semaphore_signal(
            barrier, inc=1, device_id={"seq": (me + step) % count},
            device_id_type=pl.DeviceIdType.MESH,
        )
    pl.semaphore_wait(barrier, count - 1)

    def matrix(item, index):
        source = rw_ref.at[index] if index < n_read else lw_ref.at[index - n_read]
        return Gather(source, lambda rows: w_ref.at[index, rows], shard, sems, item, spots)

    def array(item, source, ref):
        return Gather(source, lambda rows: ref.at[rows], own, sems, item, spots)

    r1, r2 = matrix(0, 1), matrix(1, 2)
    lat = array(2, lat_ref, lat_all)
    r0, l4, r3 = matrix(3, 0), matrix(4, n_read + 4), matrix(5, 3)
    l0, l1, l2 = (matrix(6 + i, n_read + i) for i in range(3))
    l3, l5, l6, l7 = (matrix(9 + i, n_read + j) for i, j in enumerate((3, 5, 6, 7)))
    kv, into = array(13, None, kv_ref), array(14, None, in_ref)

    r1.start()
    r2.start()
    lat.start()

    def norm_rows(here):
        norm_ref[here, :] = rms(tok_ref[here, :].astype(F32)).astype(BF16)

    slab = tok_ref.shape[0]
    by_rows(slab, 256, norm_rows)
    stats_ref[...] = jnp.zeros(stats_ref.shape, F32)
    r1.spread()
    r0.start()
    r2.spread()
    r1.need()

    def key_rows(here):
        k_ref[here, :] = head_norm(dot(norm_ref[here, :], w_ref[1]), group)

    by_rows(slab, 256, key_rows)
    lat.spread()
    l4.start()
    r2.need()

    def value_rows(here):
        v_ref[here, :] = dot(norm_ref[here, :], w_ref[2]).astype(BF16)

    by_rows(slab, 256, value_rows)
    lat.close()
    r0.spread()
    r3.start()
    lat.need()
    r0.need()
    l4.spread()
    l0.start()

    def query_rows(here):
        normed = rms(lat_all[here, :].astype(F32)).astype(BF16)
        q_ref[here, :] = head_norm(dot(normed, w_ref[0]), group)

    by_rows(lat_all.shape[0], 256, query_rows)

    def run(*actions):
        def body():
            for action in actions:
                action()

        return body

    attention(
        q_ref, k_ref, v_ref, scale_ref, 0, parts_ref, stats_ref, 256,
        {
            0: run(l4.close, r3.spread, l1.start),
            3: run(r3.close, l0.spread, l2.start),
            6: run(l0.close, l1.spread),
            9: run(l1.close, l2.spread),
        },
    )
    sums = []
    for step in range(1, count):
        target = (me + step) % count
        rows = pl.ds(pl.multiple_of(target * own, own), own)
        for kind, (src, dst) in enumerate(((parts_ref, got_ref), (stats_ref, got_stats))):
            copy = pltpu.make_async_remote_copy(
                src_ref=src.at[rows],
                dst_ref=dst.at[step - 1],
                send_sem=slab_send.at[step - 1, kind],
                recv_sem=slab_recv.at[step - 1, kind],
                device_id={"seq": target},
                device_id_type=pl.DeviceIdType.MESH,
            )
            copy.start()
            sums.append(copy)
    l2.close()
    l3.start()
    l4.need()

    def write_query_rows(here):
        wq_ref[here, :] = head_norm(dot(norm_ref[here, :], w_ref[n_read + 4]), group)

    by_rows(slab, 256, write_query_rows)
    for item in (r3, l0, l1, l2):
        item.need()
    for copy in sums:
        copy.wait_recv()
    mine = pl.ds(pl.multiple_of(me * own, own), own)
    combine(
        [parts_ref[mine, :]] + [got_ref[b] for b in range(count - 1)],
        [stats_ref[mine, :]] + [got_stats[b] for b in range(count - 1)],
        lat_ref, w_ref.at[3], [w_ref.at[n_read + i] for i in range(3)],
        one_ref, self_q, kv_ref.at[mine],
    )
    kv.start()
    l3.spread()
    l5.start()
    l6.start()
    l3.close()
    kv.need()
    attention(
        self_q, kv_ref.at[:, :width], kv_ref.at[:, width:], scale_ref, 1, mix_small, None, own
    )
    l3.need()
    latents_out = one_ref[...] + dot(mix_small[...], w_ref[n_read + 3])
    lat_out_ref[...] = latents_out
    in_ref[mine, :] = rms(latents_out).astype(BF16)
    into.start()
    l5.spread()
    l6.spread()
    l7.start()
    into.spread()
    l5.close()
    l6.close()
    into.need()
    l5.need()

    def write_key_rows(here):
        wk_ref[here, :] = head_norm(dot(in_ref[here, :], w_ref[n_read + 5]), group)

    def write_value_rows(here):
        wv_ref[here, :] = dot(in_ref[here, :], w_ref[n_read + 6]).astype(BF16)

    by_rows(lat_all.shape[0], 256, write_key_rows)
    l6.need()
    by_rows(lat_all.shape[0], 256, write_value_rows)
    attention(
        wq_ref, wk_ref, wv_ref, scale_ref, 2, mix_ref, None, 256,
        {2: l7.spread, 6: l7.close},
    )
    l7.need()

    def out_rows(here):
        out_ref[here, :] = (
            tok_ref[here, :].astype(F32) + dot(mix_ref[here, :], w_ref[n_read + 7])
        ).astype(out_ref.dtype)

    by_rows(slab, 256, out_rows)
    for item in (r1, r2, lat, r0, l4, r3, l0, l1, l2, l3, l5, l6, l7, kv, into):
        item.drain()
    for copy in sums:
        copy.wait_send()


def cube(count, tokens, latents, read_weights, later_weights, head_scale):
    own, width = latents.shape
    rows = own * count
    slab = tokens.shape[0]
    matrices = read_weights.shape[0] + later_weights.shape[0]
    vmem = lambda *shape: pltpu.VMEM(shape, BF16)
    full = lambda *shape: pltpu.VMEM(shape, F32)
    return pl.pallas_call(
        functools.partial(whole_body, count),
        out_shape=[
            jax.ShapeDtypeStruct(tokens.shape, BF16),
            jax.ShapeDtypeStruct(latents.shape, F32),
        ],
        in_specs=[VM, VM, pl.BlockSpec(memory_space=pl.ANY), pl.BlockSpec(memory_space=pl.ANY), SM],
        out_specs=[VM, VM],
        scratch_shapes=[
            vmem(matrices, width, width),
            vmem(slab, width),
            vmem(rows, width),
            vmem(rows, width),
            vmem(slab, width),
            vmem(slab, width),
            vmem(rows, width),
            full(rows, LANES),
            vmem(count - 1, own, width),
            full(count - 1, own, LANES),
            full(own, width),
            vmem(own, width),
            vmem(rows, 2 * width),
            vmem(own, width),
            vmem(rows, width),
            vmem(slab, width),
            vmem(rows, width),
            vmem(rows, width),
            vmem(slab, width),
            pltpu.SemaphoreType.DMA((matrices + 3, 9)),
            pltpu.SemaphoreType.DMA((matrices + 3, 8)),
            pltpu.SemaphoreType.DMA((count - 1, 2)),
            pltpu.SemaphoreType.DMA((count - 1, 2)),
        ],
        compiler_params=pltpu.CompilerParams(
            vmem_limit_bytes=60 * 1024 * 1024, collective_id=0, has_side_effects=True
        ),
    )(tokens, latents, read_weights, later_weights, head_scale)


def solution(mesh):
    placed = (
        P(("vid", "seq"), None),
        P(("vid", "seq"), None),
        P(None, "seq", None),
        P(None, "seq", None),
        P(),
    )
    count = mesh.shape["seq"]
    form = cube if count == 2**3 else gathered
    return jax.shard_map(
        functools.partial(form, count),
        mesh=mesh,
        in_specs=placed,
        out_specs=(P(("vid", "seq"), None), P(("vid", "seq"), None)),
        check_vma=False,
    )
```

```python
import functools
import math

import jax
import jax.numpy as jnp
from jax import lax
from jax.experimental import pallas as pl
from jax.experimental.pallas import tpu as pltpu
from jax.sharding import PartitionSpec as P

HEADS = 12
LANES = 128
epsilon = 1e-06
LOG2E = math.log2(math.e)
BF16 = jnp.bfloat16
F32 = jnp.float32


def rms(values):
    return values * lax.rsqrt(jnp.mean(values * values, axis=-1, keepdims=True) + epsilon)


def dot(left, right):
    return jnp.dot(left, right, preferred_element_type=F32)


def inner(left, right):
    return lax.dot_general(left, right, (((1,), (1,)), ((), ())), preferred_element_type=F32)


def group_matrix(head_dim):
    size = 2 * LANES
    row = lax.broadcasted_iota(jnp.int32, (size, size), 0) // head_dim
    col = lax.broadcasted_iota(jnp.int32, (size, size), 1) // head_dim
    return jnp.where(row == col, 1.0 / head_dim, 0.0).astype(BF16)


def head_norm(values, group):
    size = group.shape[0]
    parts = []
    for start in range(0, values.shape[1], size):
        block = values[:, start : start + size]
        square = block * block
        high = square.astype(BF16)
        low = (square - high.astype(F32)).astype(BF16)
        mean = dot(high, group) + dot(low, group)
        parts.append((block * lax.rsqrt(mean + epsilon)).astype(BF16))
    return jnp.concatenate(parts, axis=1)


def by_rows(rows, chunk, body):
    chunk = min(chunk, rows)

    def step(index, carry):
        body(pl.ds(pl.multiple_of(index * chunk, chunk), chunk))
        return carry

    lax.fori_loop(0, rows // chunk, step, 0)


def half_masks(head_dim):
    lane = lax.broadcasted_iota(jnp.int32, (1, LANES), 1) // head_dim
    return [(lane == part).astype(F32).astype(BF16) for part in range(LANES // head_dim)]


def merge_halves(parts, head_dim):
    lane = lax.broadcasted_iota(jnp.int32, parts[0].shape, 1) // head_dim
    result = parts[0]
    for part in range(1, len(parts)):
        result = jnp.where(lane == part, parts[part], result)
    return result


def attention(q_ref, k_ref, v_ref, scale_ref, which, out_ref, stats_ref, chunk, hooks=None):
    rows, width = q_ref.shape
    head_dim = width // HEADS
    per_block = LANES // head_dim
    chunk = min(chunk, rows)
    n_chunks = rows // chunk
    masks = half_masks(head_dim)
    root = 1.0 / math.sqrt(head_dim)

    def step(index, carry):
        for when, action in (hooks or {}).items():
            pl.when(index == when)(action)
        block = index // n_chunks
        part = index % n_chunks
        cols = pl.ds(pl.multiple_of(block * LANES, LANES), LANES)
        here = pl.ds(pl.multiple_of(part * chunk, chunk), chunk)
        q = q_ref[here, cols]
        k = k_ref[:, cols]
        v = v_ref[:, cols]
        results = []
        for half in range(per_block):
            head = block * per_block + half
            factor = scale_ref[which, head] * root
            scores = inner(q * masks[half], k)
            top = jnp.max(scores, axis=1, keepdims=True)
            exp_scores = jnp.exp2((scores - top) * (factor * LOG2E))
            total = jnp.sum(exp_scores, axis=1, keepdims=True)
            if stats_ref is None:
                weights = (exp_scores * (1.0 / total)).astype(BF16)
            else:
                weights = exp_scores.astype(BF16)
                lane = lax.broadcasted_iota(jnp.int32, (chunk, LANES), 1)
                old = stats_ref[here, :]
                old = jnp.where(lane == head, top * factor, old)
                stats_ref[here, :] = jnp.where(lane == head + LANES // 2, total, old)
            results.append(dot(weights, v))
        out_ref[here, cols] = merge_halves(results, head_dim).astype(BF16)
        return carry

    lax.fori_loop(0, (width // LANES) * n_chunks, step, 0)


def read_body(tok_ref, lat_ref, w_ref, scale_ref, parts_ref, stats_ref, q_ref, k_ref, v_ref):
    group = group_matrix(tok_ref.shape[1] // HEADS)

    stats_ref[...] = jnp.zeros(stats_ref.shape, F32)

    def latent_rows(here):
        normed = rms(lat_ref[here, :].astype(F32)).astype(BF16)
        q_ref[here, :] = head_norm(dot(normed, w_ref[0]), group)

    def token_rows(here):
        normed = rms(tok_ref[here, :].astype(F32)).astype(BF16)
        k_ref[here, :] = head_norm(dot(normed, w_ref[1]), group)
        v_ref[here, :] = dot(normed, w_ref[2]).astype(BF16)

    by_rows(lat_ref.shape[0], 256, latent_rows)
    by_rows(tok_ref.shape[0], 256, token_rows)
    attention(q_ref, k_ref, v_ref, scale_ref, 0, parts_ref, stats_ref, 256)


def combine(got, stats, lat_ref, out_w_ref, w_refs, one_ref, q_ref, kv_ref):
    count = len(got)
    rows, width = got[0].shape
    head_dim = width // HEADS
    group = group_matrix(head_dim)
    per_block = LANES // head_dim
    best = functools.reduce(jnp.maximum, stats)
    rescale = [jnp.exp(item - best) for item in stats]
    half = LANES // 2
    bottom = sum(rescale[b][:, :half] * stats[b][:, half:] for b in range(count))
    inverse = 1.0 / bottom
    mixed = []
    for block in range(width // LANES):
        cols = slice(block * LANES, block * LANES + LANES)
        total = jnp.zeros((rows, LANES), F32)
        heads = range(block * per_block, block * per_block + per_block)

        def spread(values):
            return merge_halves(
                [jnp.broadcast_to(values[:, h : h + 1], (rows, LANES)) for h in heads], head_dim
            )

        for b in range(count):
            total += got[b][:, cols].astype(F32) * spread(rescale[b])
        mixed.append((total * spread(inverse)).astype(BF16))
    read_mix = jnp.concatenate(mixed, axis=1)
    lat_one = lat_ref[...].astype(F32) + dot(read_mix, out_w_ref[...])
    one_ref[...] = lat_one
    normed = rms(lat_one).astype(BF16)
    q_ref[...] = head_norm(dot(normed, w_refs[0][...]), group)
    kv_ref[:, :width] = head_norm(dot(normed, w_refs[1][...]), group)
    kv_ref[:, width:] = dot(normed, w_refs[2][...]).astype(BF16)


def combine_body(got_ref, stats_ref, lat_ref, out_w_ref, w_ref, one_ref, q_ref, kv_ref):
    count = got_ref.shape[0]
    combine(
        [got_ref[b] for b in range(count)],
        [stats_ref[b] for b in range(count)],
        lat_ref, out_w_ref, [w_ref.at[i] for i in range(3)], one_ref, q_ref, kv_ref,
    )


def self_body(one_ref, q_ref, kv_ref, w_ref, scale_ref, out_ref, in_ref, mix_ref):
    width = one_ref.shape[1]
    attention(
        q_ref, kv_ref.at[:, :width], kv_ref.at[:, width:], scale_ref, 1, mix_ref, None, 64
    )
    latents_out = one_ref[...] + dot(mix_ref[...], w_ref[...])
    out_ref[...] = latents_out
    in_ref[...] = rms(latents_out).astype(BF16)


def write_body(tok_ref, in_ref, w_ref, scale_ref, out_ref, q_ref, k_ref, v_ref, mix_ref):
    group = group_matrix(tok_ref.shape[1] // HEADS)

    def latent_rows(here):
        k_ref[here, :] = head_norm(dot(in_ref[here, :], w_ref[1]), group)
        v_ref[here, :] = dot(in_ref[here, :], w_ref[2]).astype(BF16)

    def token_rows(here):
        normed = rms(tok_ref[here, :].astype(F32)).astype(BF16)
        q_ref[here, :] = head_norm(dot(normed, w_ref[0]), group)

    def out_rows(here):
        out_ref[here, :] = (
            tok_ref[here, :].astype(F32) + dot(mix_ref[here, :], w_ref[3])
        ).astype(out_ref.dtype)

    by_rows(in_ref.shape[0], 256, latent_rows)
    by_rows(tok_ref.shape[0], 256, token_rows)
    attention(q_ref, k_ref, v_ref, scale_ref, 2, mix_ref, None, 256)
    by_rows(tok_ref.shape[0], 256, out_rows)


VM = pl.BlockSpec(memory_space=pltpu.VMEM)
SM = pl.BlockSpec(memory_space=pltpu.SMEM)


def call(body, in_specs, outs, scratch, *args):
    return pl.pallas_call(
        body,
        out_shape=[jax.ShapeDtypeStruct(shape, dtype) for shape, dtype in outs],
        in_specs=in_specs,
        out_specs=[VM] * len(outs),
        scratch_shapes=[pltpu.VMEM(shape, dtype) for shape, dtype in scratch],
        compiler_params=pltpu.CompilerParams(vmem_limit_bytes=56 * 1024 * 1024),
    )(*args)


def gathered(count, tokens, latents, read_weights, later_weights, head_scale):
    own, width = latents.shape
    rows = own * count
    slab = tokens.shape[0]
    read_full = lax.all_gather(read_weights, "seq", axis=1, tiled=True)
    later_full = lax.all_gather(later_weights, "seq", axis=1, tiled=True)
    lat_all = lax.all_gather(latents, "seq", axis=0, tiled=True)
    parts, stats = call(
        read_body,
        [VM, VM, VM, SM],
        [((rows, width), BF16), ((rows, LANES), F32)],
        [((rows, width), BF16), ((slab, width), BF16), ((slab, width), BF16)],
        tokens, lat_all, read_full[:3], head_scale,
    )
    got_parts = lax.all_to_all(
        parts.reshape(count, own, width), "seq", split_axis=0, concat_axis=0, tiled=True
    )
    got_stats = lax.all_to_all(
        stats.reshape(count, own, LANES), "seq", split_axis=0, concat_axis=0, tiled=True
    )
    lat_one, self_q, self_kv = call(
        combine_body,
        [VM] * 5,
        [((own, width), F32), ((own, width), BF16), ((own, 2 * width), BF16)],
        [],
        got_parts, got_stats, latents, read_full[3], later_full[:3],
    )
    all_kv = lax.all_gather(self_kv, "seq", axis=0, tiled=True)
    latents_out, write_in = call(
        self_body,
        [VM, VM, VM, VM, SM],
        [((own, width), F32), ((own, width), BF16)],
        [((own, width), BF16)],
        lat_one, self_q, all_kv, later_full[3], head_scale,
    )
    write_all = lax.all_gather(write_in, "seq", axis=0, tiled=True)
    (tokens_out,) = call(
        write_body,
        [VM, VM, VM, SM],
        [((slab, width), BF16)],
        [((slab, width), BF16), ((rows, width), BF16), ((rows, width), BF16), ((slab, width), BF16)],
        tokens, write_all, later_full[4:], head_scale,
    )
    return tokens_out, latents_out


class Gather:
    def __init__(self, source, place, rows, sems, item, spots, pair=None):
        send, recv = sems
        me, core, along_x, along_y, diagonal = spots
        self.done = set()
        self.paired = pair is not None

        def copy(kind, src, dst, target):
            return pltpu.make_async_remote_copy(
                src_ref=src,
                dst_ref=dst,
                send_sem=send.at[item, kind],
                recv_sem=recv.at[item, kind],
                device_id=target,
                device_id_type=pl.DeviceIdType.MESH,
            )

        unit = rows // 3 if self.paired else rows // 2
        base = pair[0] * unit if self.paired else 0

        def block(owner, start=0, size=rows):
            return place(pl.ds(pl.multiple_of(owner * rows + start, unit), size))

        def both(owner, start, size):
            return block(owner, start, size), block(owner, start, size)

        x_dev, y_dev, core_dev = {"seq": along_x}, {"seq": along_y}, {"seq": core}
        mine = source if source is not None else block(me)
        share = block(me, base, 2 * unit)
        if source is None:
            part = share
        else:
            part = source.at[pl.ds(pl.multiple_of(base, unit), 2 * unit)]
        self.first = [
            copy(0, part, share, x_dev),
            copy(1, part, share, y_dev),
            copy(2, mine, block(me), core_dev),
        ]
        self.relay = [
            copy(3, *both(along_x, base, unit), y_dev),
            copy(4, *both(along_y, base + unit, unit), x_dev),
        ]
        self.forward = [
            copy(5 + i, *both(owner, 0, rows), core_dev)
            for i, owner in enumerate((along_x, along_y, diagonal))
        ]
        self.swap = []
        if self.paired:
            self.swap = [
                copy(8 + i, *both(owner, pair[0] * 2 * unit, unit), {"vid": pair[1]})
                for i, owner in enumerate((along_x, along_y, diagonal))
            ]
        self.local = None
        if source is not None:
            self.local = pltpu.make_async_copy(source, block(me), send.at[item, 11])

    def once(self, stage):
        fresh = stage not in self.done
        self.done.add(stage)
        return fresh

    def start(self):
        if self.once("start"):
            for copy in self.first:
                copy.start()
            if self.local is not None:
                self.local.start()

    def spread(self):
        if self.once("spread"):
            onward = self.swap if self.paired else self.forward
            for i in range(2):
                self.first[i].wait_recv()
                self.relay[i].start()
                onward[i].start()

    def close(self):
        if self.once("close"):
            self.relay[0].wait_recv()
            self.relay[1].wait_recv()
            (self.swap if self.paired else self.forward)[2].start()

    def settle(self):
        if self.paired and self.once("settle"):
            for i in range(3):
                self.swap[i].wait_recv()
                self.forward[i].start()

    def need(self):
        self.spread()
        self.close()
        self.settle()
        self.first[2].wait_recv()
        for copy in self.forward:
            copy.wait_recv()
        if self.local is not None:
            self.local.wait()

    def drain(self):
        for copy in self.first + self.relay + self.forward + self.swap:
            copy.wait_send()


def whole_body(
    count, tok_ref, lat_ref, rw_ref, lw_ref, scale_ref, out_ref, lat_out_ref,
    w_ref, norm_ref, lat_all, q_ref, k_ref, v_ref, parts_ref, stats_ref,
    got_ref, got_stats, one_ref, self_q, kv_ref, mix_small, in_ref,
    wq_ref, wk_ref, wv_ref, mix_ref, send, recv, slab_send, slab_recv,
):
    me = lax.axis_index("seq")
    core = me + 1 - 2 * (me % 2)
    along_x = me + 2 - 4 * ((me // 2) % 2)
    along_y = me + 4 - 8 * (me // 4)
    diagonal = along_x + 4 - 8 * (me // 4)
    spots = (me, core, along_x, along_y, diagonal)
    own, width = lat_ref.shape
    n_read = rw_ref.shape[0]
    shard = rw_ref.shape[1]
    group = group_matrix(width // HEADS)
    sems = (send, recv)

    barrier = pltpu.get_barrier_semaphore()
    for step in range(1, count):
        pl.semaphore_signal(
            barrier, inc=1, device_id={"seq": (me + step) % count},
            device_id_type=pl.DeviceIdType.MESH,
        )
    plane = lax.axis_index("vid")
    pair = (plane % 2, plane + 1 - 2 * (plane % 2))
    pl.semaphore_signal(
        barrier, inc=1, device_id={"vid": pair[1]}, device_id_type=pl.DeviceIdType.MESH
    )
    pl.semaphore_wait(barrier, count)

    def matrix(item, index):
        source = rw_ref.at[index] if index < n_read else lw_ref.at[index - n_read]
        return Gather(source, lambda rows: w_ref.at[index, rows], shard, sems, item, spots, pair)

    def array(item, source, ref):
        return Gather(source, lambda rows: ref.at[rows], own, sems, item, spots)

    r1, r2 = matrix(0, 1), matrix(1, 2)
    lat = array(2, lat_ref, lat_all)
    r0, l4, r3 = matrix(3, 0), matrix(4, n_read + 4), matrix(5, 3)
    l0, l1, l2 = (matrix(6 + i, n_read + i) for i in range(3))
    l3, l5, l6, l7 = (matrix(9 + i, n_read + j) for i, j in enumerate((3, 5, 6, 7)))
    kv, into = array(13, None, kv_ref), array(14, None, in_ref)

    r1.start()
    r2.start()
    lat.start()

    def norm_rows(here):
        norm_ref[here, :] = rms(tok_ref[here, :].astype(F32)).astype(BF16)

    slab = tok_ref.shape[0]
    by_rows(slab, 256, norm_rows)
    stats_ref[...] = jnp.zeros(stats_ref.shape, F32)
    r1.spread()
    r0.start()
    r1.close()
    r2.spread()
    l4.start()
    r2.close()
    r1.need()

    def key_rows(here):
        k_ref[here, :] = head_norm(dot(norm_ref[here, :], w_ref[1]), group)

    by_rows(slab, 256, key_rows)
    lat.spread()
    r3.start()
    r2.need()

    def value_rows(here):
        v_ref[here, :] = dot(norm_ref[here, :], w_ref[2]).astype(BF16)

    by_rows(slab, 256, value_rows)
    lat.close()
    r0.spread()
    l0.start()
    r0.close()
    l4.spread()
    lat.need()
    r0.need()
    l4.close()

    def query_rows(here):
        normed = rms(lat_all[here, :].astype(F32)).astype(BF16)
        q_ref[here, :] = head_norm(dot(normed, w_ref[0]), group)

    by_rows(lat_all.shape[0], 256, query_rows)

    def run(*actions):
        def body():
            for action in actions:
                action()

        return body

    sums = []

    def exchange(src, dst, cols, kind):
        copies = []
        for step in range(1, count):
            target = (me + step) % count
            rows = pl.ds(pl.multiple_of(target * own, own), own)
            copies.append(
                pltpu.make_async_remote_copy(
                    src_ref=src.at[rows, cols],
                    dst_ref=dst.at[step - 1, :, cols],
                    send_sem=slab_send.at[step - 1, kind],
                    recv_sem=slab_recv.at[step - 1, kind],
                    device_id={"seq": target},
                    device_id_type=pl.DeviceIdType.MESH,
                )
            )
        sums.extend(copies)

        def body():
            for copy in copies:
                copy.start()

        return body

    third = width // 3
    groups = [
        exchange(parts_ref, got_ref, slice(i * third, i * third + third), i) for i in range(3)
    ]
    attention(
        q_ref, k_ref, v_ref, scale_ref, 0, parts_ref, stats_ref, lat_all.shape[0] // 2,
        {
            0: run(l4.settle, r3.spread, l1.start),
            2: run(r3.close, l0.spread, l2.start),
            4: run(groups[0], r3.settle, l0.close, l1.spread, l3.start),
            6: run(l0.settle, l1.close, l2.spread, l5.start),
            8: run(groups[1], l1.settle, l2.close, l3.spread, l6.start),
            10: run(l2.settle, l3.close, l5.spread, l7.start),
        },
    )
    groups[2]()
    exchange(stats_ref, got_stats, slice(0, LANES), 3)()
    l3.settle()
    l5.close()
    l6.spread()
    l4.need()

    def write_query_rows(here):
        wq_ref[here, :] = head_norm(dot(norm_ref[here, :], w_ref[n_read + 4]), group)

    by_rows(slab, 256, write_query_rows)
    l5.settle()
    l6.close()
    l7.spread()
    for item in (r3, l0, l1, l2):
        item.need()
    for copy in sums:
        copy.wait_recv()
    mine = pl.ds(pl.multiple_of(me * own, own), own)
    combine(
        [parts_ref[mine, :]] + [got_ref[b] for b in range(count - 1)],
        [stats_ref[mine, :]] + [got_stats[b] for b in range(count - 1)],
        lat_ref, w_ref.at[3], [w_ref.at[n_read + i] for i in range(3)],
        one_ref, self_q, kv_ref.at[mine],
    )
    kv.start()
    l6.settle()
    l7.close()
    kv.need()
    attention(
        self_q, kv_ref.at[:, :width], kv_ref.at[:, width:], scale_ref, 1, mix_small, None, own
    )
    l3.need()
    latents_out = one_ref[...] + dot(mix_small[...], w_ref[n_read + 3])
    lat_out_ref[...] = latents_out
    in_ref[mine, :] = rms(latents_out).astype(BF16)
    into.start()
    l7.settle()
    into.need()
    l5.need()

    def write_key_rows(here):
        wk_ref[here, :] = head_norm(dot(in_ref[here, :], w_ref[n_read + 5]), group)

    def write_value_rows(here):
        wv_ref[here, :] = dot(in_ref[here, :], w_ref[n_read + 6]).astype(BF16)

    by_rows(lat_all.shape[0], 256, write_key_rows)
    l6.need()
    by_rows(lat_all.shape[0], 256, write_value_rows)
    attention(
        wq_ref, wk_ref, wv_ref, scale_ref, 2, mix_ref, None, 256
    )
    l7.need()

    def out_rows(here):
        out_ref[here, :] = (
            tok_ref[here, :].astype(F32) + dot(mix_ref[here, :], w_ref[n_read + 7])
        ).astype(out_ref.dtype)

    by_rows(slab, 256, out_rows)
    for item in (r1, r2, lat, r0, l4, r3, l0, l1, l2, l3, l5, l6, l7, kv, into):
        item.drain()
    for copy in sums:
        copy.wait_send()


def cube(count, tokens, latents, read_weights, later_weights, head_scale):
    own, width = latents.shape
    rows = own * count
    slab = tokens.shape[0]
    matrices = read_weights.shape[0] + later_weights.shape[0]
    vmem = lambda *shape: pltpu.VMEM(shape, BF16)
    full = lambda *shape: pltpu.VMEM(shape, F32)
    return pl.pallas_call(
        functools.partial(whole_body, count),
        out_shape=[
            jax.ShapeDtypeStruct(tokens.shape, BF16),
            jax.ShapeDtypeStruct(latents.shape, F32),
        ],
        in_specs=[VM, VM, pl.BlockSpec(memory_space=pl.ANY), pl.BlockSpec(memory_space=pl.ANY), SM],
        out_specs=[VM, VM],
        scratch_shapes=[
            vmem(matrices, width, width),
            vmem(slab, width),
            vmem(rows, width),
            vmem(rows, width),
            vmem(slab, width),
            vmem(slab, width),
            vmem(rows, width),
            full(rows, LANES),
            vmem(count - 1, own, width),
            full(count - 1, own, LANES),
            full(own, width),
            vmem(own, width),
            vmem(rows, 2 * width),
            vmem(own, width),
            vmem(rows, width),
            vmem(slab, width),
            vmem(rows, width),
            vmem(rows, width),
            vmem(slab, width),
            pltpu.SemaphoreType.DMA((matrices + 3, 12)),
            pltpu.SemaphoreType.DMA((matrices + 3, 11)),
            pltpu.SemaphoreType.DMA((count - 1, 4)),
            pltpu.SemaphoreType.DMA((count - 1, 4)),
        ],
        compiler_params=pltpu.CompilerParams(
            vmem_limit_bytes=60 * 1024 * 1024, collective_id=0, has_side_effects=True
        ),
    )(tokens, latents, read_weights, later_weights, head_scale)


def solution(mesh):
    placed = (
        P(("vid", "seq"), None),
        P(("vid", "seq"), None),
        P(None, "seq", None),
        P(None, "seq", None),
        P(),
    )
    count = mesh.shape["seq"]
    form = cube if count == 2**3 and mesh.shape["vid"] % 2 == 0 else gathered
    return jax.shard_map(
        functools.partial(form, count),
        mesh=mesh,
        in_specs=placed,
        out_specs=(P(("vid", "seq"), None), P(("vid", "seq"), None)),
        check_vma=False,
    )
```

```python
import functools
import math

import jax
import jax.numpy as jnp
from jax import lax
from jax.experimental import pallas as pl
from jax.experimental.pallas import tpu as pltpu
from jax.sharding import PartitionSpec as P

HEADS = 12
LANES = 128
epsilon = 1e-06
LOG2E = math.log2(math.e)
BF16 = jnp.bfloat16
F32 = jnp.float32


def rms(values):
    return values * lax.rsqrt(jnp.mean(values * values, axis=-1, keepdims=True) + epsilon)


def dot(left, right):
    return jnp.dot(left, right, preferred_element_type=F32)


def inner(left, right):
    return lax.dot_general(left, right, (((1,), (1,)), ((), ())), preferred_element_type=F32)


def group_matrix(head_dim):
    size = 2 * LANES
    row = lax.broadcasted_iota(jnp.int32, (size, size), 0) // head_dim
    col = lax.broadcasted_iota(jnp.int32, (size, size), 1) // head_dim
    return jnp.where(row == col, 1.0 / head_dim, 0.0).astype(BF16)


def head_norm(values, group):
    size = group.shape[0]
    parts = []
    for start in range(0, values.shape[1], size):
        block = values[:, start : start + size]
        square = block * block
        high = square.astype(BF16)
        low = (square - high.astype(F32)).astype(BF16)
        mean = dot(high, group) + dot(low, group)
        parts.append((block * lax.rsqrt(mean + epsilon)).astype(BF16))
    return jnp.concatenate(parts, axis=1)


def by_rows(rows, chunk, body):
    chunk = min(chunk, rows)

    def step(index, carry):
        body(pl.ds(pl.multiple_of(index * chunk, chunk), chunk))
        return carry

    lax.fori_loop(0, rows // chunk, step, 0)


def half_masks(head_dim):
    lane = lax.broadcasted_iota(jnp.int32, (1, LANES), 1) // head_dim
    return [(lane == part).astype(F32).astype(BF16) for part in range(LANES // head_dim)]


def merge_halves(parts, head_dim):
    lane = lax.broadcasted_iota(jnp.int32, parts[0].shape, 1) // head_dim
    result = parts[0]
    for part in range(1, len(parts)):
        result = jnp.where(lane == part, parts[part], result)
    return result


def attention(q_ref, k_ref, v_ref, scale_ref, which, out_ref, stats_ref, chunk, hooks=None):
    rows, width = q_ref.shape
    head_dim = width // HEADS
    per_block = LANES // head_dim
    chunk = min(chunk, rows)
    n_chunks = rows // chunk
    masks = half_masks(head_dim)
    root = 1.0 / math.sqrt(head_dim)

    def step(index, carry):
        for when, action in (hooks or {}).items():
            pl.when(index == when)(action)
        block = index // n_chunks
        part = index % n_chunks
        cols = pl.ds(pl.multiple_of(block * LANES, LANES), LANES)
        here = pl.ds(pl.multiple_of(part * chunk, chunk), chunk)
        q = q_ref[here, cols]
        k = k_ref[:, cols]
        v = v_ref[:, cols]
        results = []
        for half in range(per_block):
            head = block * per_block + half
            factor = scale_ref[which, head] * root
            scores = inner(q * masks[half], k)
            top = jnp.max(scores, axis=1, keepdims=True)
            exp_scores = jnp.exp2((scores - top) * (factor * LOG2E))
            total = jnp.sum(exp_scores, axis=1, keepdims=True)
            weights = exp_scores.astype(BF16)
            if stats_ref is not None:
                lane = lax.broadcasted_iota(jnp.int32, (chunk, LANES), 1)
                old = stats_ref[here, :]
                old = jnp.where(lane == head, top * factor, old)
                stats_ref[here, :] = jnp.where(lane == head + LANES // 2, total, old)
            mixed = dot(weights, v)
            results.append(mixed / total if stats_ref is None else mixed)
        out_ref[here, cols] = merge_halves(results, head_dim).astype(BF16)
        return carry

    lax.fori_loop(0, (width // LANES) * n_chunks, step, 0)


def read_body(tok_ref, lat_ref, w_ref, scale_ref, parts_ref, stats_ref, q_ref, k_ref, v_ref):
    group = group_matrix(tok_ref.shape[1] // HEADS)

    stats_ref[...] = jnp.zeros(stats_ref.shape, F32)

    def latent_rows(here):
        normed = rms(lat_ref[here, :].astype(F32)).astype(BF16)
        q_ref[here, :] = head_norm(dot(normed, w_ref[0]), group)

    def token_rows(here):
        normed = rms(tok_ref[here, :].astype(F32)).astype(BF16)
        k_ref[here, :] = head_norm(dot(normed, w_ref[1]), group)
        v_ref[here, :] = dot(normed, w_ref[2]).astype(BF16)

    by_rows(lat_ref.shape[0], 256, latent_rows)
    by_rows(tok_ref.shape[0], 256, token_rows)
    attention(q_ref, k_ref, v_ref, scale_ref, 0, parts_ref, stats_ref, 256)


def combine(got, stats, lat_ref, out_w_ref, w_refs, one_ref, q_ref, kv_ref):
    count = len(got)
    rows, width = got[0].shape
    head_dim = width // HEADS
    group = group_matrix(head_dim)
    per_block = LANES // head_dim
    best = functools.reduce(jnp.maximum, stats)
    rescale = [jnp.exp(item - best) for item in stats]
    half = LANES // 2
    bottom = sum(rescale[b][:, :half] * stats[b][:, half:] for b in range(count))
    inverse = 1.0 / bottom
    mixed = []
    for block in range(width // LANES):
        cols = slice(block * LANES, block * LANES + LANES)
        total = jnp.zeros((rows, LANES), F32)
        heads = range(block * per_block, block * per_block + per_block)

        def spread(values):
            return merge_halves(
                [jnp.broadcast_to(values[:, h : h + 1], (rows, LANES)) for h in heads], head_dim
            )

        for b in range(count):
            total += got[b][:, cols].astype(F32) * spread(rescale[b])
        mixed.append((total * spread(inverse)).astype(BF16))
    read_mix = jnp.concatenate(mixed, axis=1)
    lat_one = lat_ref[...].astype(F32) + dot(read_mix, out_w_ref[...])
    one_ref[...] = lat_one
    normed = rms(lat_one).astype(BF16)
    q_ref[...] = head_norm(dot(normed, w_refs[0][...]), group)
    kv_ref[:, :width] = head_norm(dot(normed, w_refs[1][...]), group)
    kv_ref[:, width:] = dot(normed, w_refs[2][...]).astype(BF16)


def combine_body(got_ref, stats_ref, lat_ref, out_w_ref, w_ref, one_ref, q_ref, kv_ref):
    count = got_ref.shape[0]
    combine(
        [got_ref[b] for b in range(count)],
        [stats_ref[b] for b in range(count)],
        lat_ref, out_w_ref, [w_ref.at[i] for i in range(3)], one_ref, q_ref, kv_ref,
    )


def self_body(one_ref, q_ref, kv_ref, w_ref, scale_ref, out_ref, in_ref, mix_ref):
    width = one_ref.shape[1]
    attention(
        q_ref, kv_ref.at[:, :width], kv_ref.at[:, width:], scale_ref, 1, mix_ref, None, 64
    )
    latents_out = one_ref[...] + dot(mix_ref[...], w_ref[...])
    out_ref[...] = latents_out
    in_ref[...] = rms(latents_out).astype(BF16)


def write_body(tok_ref, in_ref, w_ref, scale_ref, out_ref, q_ref, k_ref, v_ref, mix_ref):
    group = group_matrix(tok_ref.shape[1] // HEADS)

    def latent_rows(here):
        k_ref[here, :] = head_norm(dot(in_ref[here, :], w_ref[1]), group)
        v_ref[here, :] = dot(in_ref[here, :], w_ref[2]).astype(BF16)

    def token_rows(here):
        normed = rms(tok_ref[here, :].astype(F32)).astype(BF16)
        q_ref[here, :] = head_norm(dot(normed, w_ref[0]), group)

    def out_rows(here):
        out_ref[here, :] = (
            tok_ref[here, :].astype(F32) + dot(mix_ref[here, :], w_ref[3])
        ).astype(out_ref.dtype)

    by_rows(in_ref.shape[0], 256, latent_rows)
    by_rows(tok_ref.shape[0], 256, token_rows)
    attention(q_ref, k_ref, v_ref, scale_ref, 2, mix_ref, None, 256)
    by_rows(tok_ref.shape[0], 256, out_rows)


VM = pl.BlockSpec(memory_space=pltpu.VMEM)
SM = pl.BlockSpec(memory_space=pltpu.SMEM)


def call(body, in_specs, outs, scratch, *args):
    return pl.pallas_call(
        body,
        out_shape=[jax.ShapeDtypeStruct(shape, dtype) for shape, dtype in outs],
        in_specs=in_specs,
        out_specs=[VM] * len(outs),
        scratch_shapes=[pltpu.VMEM(shape, dtype) for shape, dtype in scratch],
        compiler_params=pltpu.CompilerParams(vmem_limit_bytes=56 * 1024 * 1024),
    )(*args)


def gathered(count, tokens, latents, read_weights, later_weights, head_scale):
    own, width = latents.shape
    rows = own * count
    slab = tokens.shape[0]
    read_full = lax.all_gather(read_weights, "seq", axis=1, tiled=True)
    later_full = lax.all_gather(later_weights, "seq", axis=1, tiled=True)
    lat_all = lax.all_gather(latents, "seq", axis=0, tiled=True)
    parts, stats = call(
        read_body,
        [VM, VM, VM, SM],
        [((rows, width), BF16), ((rows, LANES), F32)],
        [((rows, width), BF16), ((slab, width), BF16), ((slab, width), BF16)],
        tokens, lat_all, read_full[:3], head_scale,
    )
    got_parts = lax.all_to_all(
        parts.reshape(count, own, width), "seq", split_axis=0, concat_axis=0, tiled=True
    )
    got_stats = lax.all_to_all(
        stats.reshape(count, own, LANES), "seq", split_axis=0, concat_axis=0, tiled=True
    )
    lat_one, self_q, self_kv = call(
        combine_body,
        [VM] * 5,
        [((own, width), F32), ((own, width), BF16), ((own, 2 * width), BF16)],
        [],
        got_parts, got_stats, latents, read_full[3], later_full[:3],
    )
    all_kv = lax.all_gather(self_kv, "seq", axis=0, tiled=True)
    latents_out, write_in = call(
        self_body,
        [VM, VM, VM, VM, SM],
        [((own, width), F32), ((own, width), BF16)],
        [((own, width), BF16)],
        lat_one, self_q, all_kv, later_full[3], head_scale,
    )
    write_all = lax.all_gather(write_in, "seq", axis=0, tiled=True)
    (tokens_out,) = call(
        write_body,
        [VM, VM, VM, SM],
        [((slab, width), BF16)],
        [((slab, width), BF16), ((rows, width), BF16), ((rows, width), BF16), ((slab, width), BF16)],
        tokens, write_all, later_full[4:], head_scale,
    )
    return tokens_out, latents_out


class Gather:
    def __init__(self, source, place, rows, sems, item, spots, pair=None):
        send, recv = sems
        me, core, along_x, along_y, diagonal = spots
        self.done = set()
        self.paired = pair is not None

        def copy(kind, src, dst, target):
            return pltpu.make_async_remote_copy(
                src_ref=src,
                dst_ref=dst,
                send_sem=send.at[item, kind],
                recv_sem=recv.at[item, kind],
                device_id=target,
                device_id_type=pl.DeviceIdType.MESH,
            )

        unit = rows // 3 if self.paired else rows // 2
        base = pair[0] * unit if self.paired else 0

        def block(owner, start=0, size=rows):
            return place(pl.ds(pl.multiple_of(owner * rows + start, unit), size))

        def both(owner, start, size):
            return block(owner, start, size), block(owner, start, size)

        x_dev, y_dev, core_dev = {"seq": along_x}, {"seq": along_y}, {"seq": core}
        mine = source if source is not None else block(me)
        share = block(me, base, 2 * unit)
        if source is None:
            part = share
        else:
            part = source.at[pl.ds(pl.multiple_of(base, unit), 2 * unit)]
        self.first = [
            copy(0, part, share, x_dev),
            copy(1, part, share, y_dev),
            copy(2, mine, block(me), core_dev),
        ]
        self.relay = [
            copy(3, *both(along_x, base, unit), y_dev),
            copy(4, *both(along_y, base + unit, unit), x_dev),
        ]
        self.forward = [
            copy(5 + i, *both(owner, 0, rows), core_dev)
            for i, owner in enumerate((along_x, along_y, diagonal))
        ]
        self.swap = []
        if self.paired:
            self.swap = [
                copy(8 + i, *both(owner, pair[0] * 2 * unit, unit), {"vid": pair[1]})
                for i, owner in enumerate((along_x, along_y, diagonal))
            ]
        self.local = None
        if source is not None:
            self.local = pltpu.make_async_copy(source, block(me), send.at[item, 11])

    def once(self, stage):
        fresh = stage not in self.done
        self.done.add(stage)
        return fresh

    def start(self):
        if self.once("start"):
            for copy in self.first:
                copy.start()
            if self.local is not None:
                self.local.start()

    def spread(self):
        if self.once("spread"):
            onward = self.swap if self.paired else self.forward
            for i in range(2):
                self.first[i].wait_recv()
                self.relay[i].start()
                onward[i].start()

    def close(self):
        if self.once("close"):
            self.relay[0].wait_recv()
            self.relay[1].wait_recv()
            (self.swap if self.paired else self.forward)[2].start()

    def settle(self):
        if self.paired and self.once("settle"):
            for i in range(3):
                self.swap[i].wait_recv()
                self.forward[i].start()

    def need(self):
        self.spread()
        self.close()
        self.settle()
        self.first[2].wait_recv()
        for copy in self.forward:
            copy.wait_recv()
        if self.local is not None:
            self.local.wait()

    def drain(self):
        for copy in self.first + self.relay + self.forward + self.swap:
            copy.wait_send()


def whole_body(
    count, tok_ref, lat_ref, rw_ref, lw_ref, scale_ref, out_ref, lat_out_ref,
    w_ref, norm_ref, lat_all, q_ref, k_ref, v_ref, parts_ref, stats_ref,
    got_ref, got_stats, one_ref, self_q, kv_ref, mix_small, in_ref,
    wq_ref, wk_ref, wv_ref, mix_ref, send, recv, slab_send, slab_recv,
):
    me = lax.axis_index("seq")
    core = me + 1 - 2 * (me % 2)
    along_x = me + 2 - 4 * ((me // 2) % 2)
    along_y = me + 4 - 8 * (me // 4)
    diagonal = along_x + 4 - 8 * (me // 4)
    spots = (me, core, along_x, along_y, diagonal)
    own, width = lat_ref.shape
    n_read = rw_ref.shape[0]
    shard = rw_ref.shape[1]
    group = group_matrix(width // HEADS)
    sems = (send, recv)

    barrier = pltpu.get_barrier_semaphore()
    for step in range(1, count):
        pl.semaphore_signal(
            barrier, inc=1, device_id={"seq": (me + step) % count},
            device_id_type=pl.DeviceIdType.MESH,
        )
    plane = lax.axis_index("vid")
    pair = (plane % 2, plane + 1 - 2 * (plane % 2))
    pl.semaphore_signal(
        barrier, inc=1, device_id={"vid": pair[1]}, device_id_type=pl.DeviceIdType.MESH
    )
    pl.semaphore_wait(barrier, count)

    def matrix(item, index):
        source = rw_ref.at[index] if index < n_read else lw_ref.at[index - n_read]
        return Gather(source, lambda rows: w_ref.at[index, rows], shard, sems, item, spots, pair)

    def array(item, source, ref):
        return Gather(source, lambda rows: ref.at[rows], own, sems, item, spots)

    r1, r2 = matrix(0, 1), matrix(1, 2)
    lat = array(2, lat_ref, lat_all)
    r0, l4, r3 = matrix(3, 0), matrix(4, n_read + 4), matrix(5, 3)
    l0, l1, l2 = (matrix(6 + i, n_read + i) for i in range(3))
    l3, l5, l6, l7 = (matrix(9 + i, n_read + j) for i, j in enumerate((3, 5, 6, 7)))
    kv, into = array(13, None, kv_ref), array(14, None, in_ref)

    r1.start()
    r2.start()
    lat.start()
    r0.start()

    def norm_rows(here):
        norm_ref[here, :] = rms(tok_ref[here, :].astype(F32)).astype(BF16)

    slab = tok_ref.shape[0]
    by_rows(slab, 256, norm_rows)
    stats_ref[...] = jnp.zeros(stats_ref.shape, F32)
    r1.spread()
    l4.start()
    r1.close()
    r2.spread()
    r3.start()
    r2.close()
    r1.need()

    def key_rows(here):
        k_ref[here, :] = head_norm(dot(norm_ref[here, :], w_ref[1]), group)

    by_rows(slab, 256, key_rows)
    lat.spread()
    l0.start()
    r2.need()

    def value_rows(here):
        v_ref[here, :] = dot(norm_ref[here, :], w_ref[2]).astype(BF16)

    by_rows(slab, 256, value_rows)
    lat.close()
    r0.spread()
    l1.start()
    r0.close()
    l4.spread()
    lat.need()
    r0.need()
    l4.close()

    def query_rows(here):
        normed = rms(lat_all[here, :].astype(F32)).astype(BF16)
        q_ref[here, :] = head_norm(dot(normed, w_ref[0]), group)

    by_rows(lat_all.shape[0], 256, query_rows)

    def run(*actions):
        def body():
            for action in actions:
                action()

        return body

    sums = []

    def exchange(src, dst, cols, kind):
        copies = []
        for step in range(1, count):
            target = (me + step) % count
            rows = pl.ds(pl.multiple_of(target * own, own), own)
            copies.append(
                pltpu.make_async_remote_copy(
                    src_ref=src.at[rows, cols],
                    dst_ref=dst.at[step - 1, :, cols],
                    send_sem=slab_send.at[step - 1, kind],
                    recv_sem=slab_recv.at[step - 1, kind],
                    device_id={"seq": target},
                    device_id_type=pl.DeviceIdType.MESH,
                )
            )
        sums.extend(copies)

        def body():
            for copy in copies:
                copy.start()

        return body

    third = width // 3
    groups = [
        exchange(parts_ref, got_ref, slice(i * third, i * third + third), i) for i in range(3)
    ]
    attention(
        q_ref, k_ref, v_ref, scale_ref, 0, parts_ref, stats_ref, lat_all.shape[0] // 2,
        {
            0: run(l4.settle, r3.spread, l2.start),
            2: run(r3.close, l0.spread, l3.start),
            4: run(groups[0], r3.settle, l0.close, l1.spread, l5.start),
            6: run(l0.settle, l1.close, l2.spread, l6.start),
            8: run(groups[1], l1.settle, l2.close, l3.spread, l7.start),
            10: run(l2.settle, l3.close, l5.spread),
        },
    )
    groups[2]()
    exchange(stats_ref, got_stats, slice(0, LANES), 3)()
    l3.settle()
    l5.close()
    l6.spread()
    l4.need()

    def write_query_rows(here):
        wq_ref[here, :] = head_norm(dot(norm_ref[here, :], w_ref[n_read + 4]), group)

    by_rows(slab, 256, write_query_rows)
    l5.settle()
    l6.close()
    l7.spread()
    for item in (r3, l0, l1, l2):
        item.need()
    for copy in sums:
        copy.wait_recv()
    mine = pl.ds(pl.multiple_of(me * own, own), own)
    combine(
        [parts_ref[mine, :]] + [got_ref[b] for b in range(count - 1)],
        [stats_ref[mine, :]] + [got_stats[b] for b in range(count - 1)],
        lat_ref, w_ref.at[3], [w_ref.at[n_read + i] for i in range(3)],
        one_ref, self_q, kv_ref.at[mine],
    )
    kv.start()
    l6.settle()
    l7.close()
    kv.need()
    attention(
        self_q, kv_ref.at[:, :width], kv_ref.at[:, width:], scale_ref, 1, mix_small, None, own
    )
    l3.need()
    latents_out = one_ref[...] + dot(mix_small[...], w_ref[n_read + 3])
    lat_out_ref[...] = latents_out
    in_ref[mine, :] = rms(latents_out).astype(BF16)
    into.start()
    l7.settle()
    into.need()
    l5.need()

    def write_key_rows(here):
        wk_ref[here, :] = head_norm(dot(in_ref[here, :], w_ref[n_read + 5]), group)

    def write_value_rows(here):
        wv_ref[here, :] = dot(in_ref[here, :], w_ref[n_read + 6]).astype(BF16)

    by_rows(lat_all.shape[0], 256, write_key_rows)
    l6.need()
    by_rows(lat_all.shape[0], 256, write_value_rows)
    attention(
        wq_ref, wk_ref, wv_ref, scale_ref, 2, mix_ref, None, 256
    )
    l7.need()

    def out_rows(here):
        out_ref[here, :] = (
            tok_ref[here, :].astype(F32) + dot(mix_ref[here, :], w_ref[n_read + 7])
        ).astype(out_ref.dtype)

    by_rows(slab, 256, out_rows)
    for item in (r1, r2, lat, r0, l4, r3, l0, l1, l2, l3, l5, l6, l7, kv, into):
        item.drain()
    for copy in sums:
        copy.wait_send()


def cube(count, tokens, latents, read_weights, later_weights, head_scale):
    own, width = latents.shape
    rows = own * count
    slab = tokens.shape[0]
    matrices = read_weights.shape[0] + later_weights.shape[0]
    vmem = lambda *shape: pltpu.VMEM(shape, BF16)
    full = lambda *shape: pltpu.VMEM(shape, F32)
    return pl.pallas_call(
        functools.partial(whole_body, count),
        out_shape=[
            jax.ShapeDtypeStruct(tokens.shape, BF16),
            jax.ShapeDtypeStruct(latents.shape, F32),
        ],
        in_specs=[VM, VM, pl.BlockSpec(memory_space=pl.ANY), pl.BlockSpec(memory_space=pl.ANY), SM],
        out_specs=[VM, VM],
        scratch_shapes=[
            vmem(matrices, width, width),
            vmem(slab, width),
            vmem(rows, width),
            vmem(rows, width),
            vmem(slab, width),
            vmem(slab, width),
            vmem(rows, width),
            full(rows, LANES),
            vmem(count - 1, own, width),
            full(count - 1, own, LANES),
            full(own, width),
            vmem(own, width),
            vmem(rows, 2 * width),
            vmem(own, width),
            vmem(rows, width),
            vmem(slab, width),
            vmem(rows, width),
            vmem(rows, width),
            vmem(slab, width),
            pltpu.SemaphoreType.DMA((matrices + 3, 12)),
            pltpu.SemaphoreType.DMA((matrices + 3, 11)),
            pltpu.SemaphoreType.DMA((count - 1, 4)),
            pltpu.SemaphoreType.DMA((count - 1, 4)),
        ],
        compiler_params=pltpu.CompilerParams(
            vmem_limit_bytes=60 * 1024 * 1024, collective_id=0, has_side_effects=True
        ),
    )(tokens, latents, read_weights, later_weights, head_scale)


def solution(mesh):
    placed = (
        P(("vid", "seq"), None),
        P(("vid", "seq"), None),
        P(None, "seq", None),
        P(None, "seq", None),
        P(),
    )
    count = mesh.shape["seq"]
    form = cube if count == 2**3 and mesh.shape["vid"] % 2 == 0 else gathered
    return jax.shard_map(
        functools.partial(form, count),
        mesh=mesh,
        in_specs=placed,
        out_specs=(P(("vid", "seq"), None), P(("vid", "seq"), None)),
        check_vma=False,
    )
```
